256 devices in a mesh: rep: 16 (over x, z_hi), tp: 16 (over z_lo, y, core).
Axes of the slice: x: 4, y: 4, z: 8 (z_hi: 4, z_lo: 2; z = z_hi * 2 + z_lo), core: 2. Of those that a mesh axis runs over, the one named last changes fastest.
Arguments:
- hidden: bfloat16 [32768, 8192], P('rep', 'tp'), may hold values from -0.0625 to 0.0625
- target: bfloat16 [32768, 1024], P('rep'), may hold values from -6 to 6
- inner_weight: bfloat16 [16, 8192, 1024], P('rep', 'tp'), as said below
- first_moment: float32 [16, 8192, 1024], P('rep', 'tp'), may hold values from -1.5 to 1.5
- second_moment: float32 [16, 8192, 1024], P('rep', 'tp'), may hold values from 0.001 to 0.01
- anchor: float32 [16, 512, 1024], P('tp', 'rep')
- outer_momentum: float32 [16, 512, 1024], P('tp', 'rep'), may hold values from -1.5 to 1.5
Outputs:
- fragment: bfloat16 [8192, 1024], P('tp')
- momentum_new: float32 [16, 512, 1024], P('tp', 'rep')
The draws below stay inside these ranges and needn't reach their ends.
Inputs may be any that keep to these rules, and one draw needn't show every extreme that they name: `inner_weight`: each replica's inner weights are the anchor plus a drift of their own.
All inputs are finite; a program needn't handle non-finite values.
Results may differ from the reference program's by a relative error of at most 0.0017.
Values may be sent and summed in bfloat16 or wider, within the bound.
No kernel may reach another device: no remote copies, remote signals or barrier semaphores. Data moves between devices by JAX's collectives and lax.ppermute only.
A program may use at most 64 MiB of HBM per device.

```python
import math
import jax
import jax.numpy as jnp
from jax import lax

D = 8192
KVW = 1024
TOK = 2048
REPS = 16
ROWS = 512
TOKENS = 32768
N_TP = 16


def shared_base(key):
    inner_key = jax.random.fold_in(key, 11)
    base = jax.random.normal(inner_key, (D, KVW), jnp.float32)
    return base


def draw_anchor(key, part):
    return shared_base(key).reshape(N_TP, ROWS, KVW)


def draw_inner_weight(key, part):
    base = shared_base(key)
    drift = 0.1 * jax.random.normal(jax.random.fold_in(key, 12), (REPS, D, KVW), jnp.float32)
    return (base[None, :, :] + drift).astype(jnp.bfloat16)


def levels(key, shape, split, least, top_value):
    factor_of = 1.0
    for axis_at, parts in split:
        heights = jax.random.uniform(jax.random.fold_in(jax.random.fold_in(key, 6), axis_at), (parts,), jnp.float32, least / len(split), top_value / len(split))
        factor_of = factor_of * jnp.repeat(jnp.exp(heights), shape[axis_at] // parts).reshape((-1,) + (1,) * (len(shape) - 1 - axis_at))
    return factor_of


def centred(key, extent, deviation, most, split=(), held_as=jnp.bfloat16):
    values = jax.random.normal(key, extent, jnp.float32) * deviation
    if len(split) > 0:
        values = levels(key, extent, split, -0.22, 0.18) * values
    return jnp.clip(values, min=-most, max=most).astype(held_as)


def setup_inputs(seed: int = 0) -> dict:
    key_of = jax.random.split(jax.random.key(seed), 8)
    return {
        "hidden": centred(key_of[0], (TOKENS, D), D ** -0.5, 0.0625, ((0, 16), (1, 16))),
        "target": centred(key_of[1], (TOKENS, KVW), 1.0, 6.0, ((0, 16),)),
        "inner_weight": draw_inner_weight(jax.random.fold_in(key_of[7], 71), 0),
        "first_moment": centred(key_of[3], (REPS, D, KVW), 0.1, 1.5, ((0, 16), (1, 16)), jnp.float32),
        "second_moment": jnp.clip(jnp.exp(math.log(0.01) - 2.30258502 * jax.random.uniform(key_of[4], (REPS, D, KVW), jnp.float32) ** levels(key_of[4], (REPS, D, KVW), ((0, 16), (1, 16)), -0.2, 0.2)), 0.001, 0.01),
        "anchor": draw_anchor(jax.random.fold_in(key_of[7], 71), 0),
        "outer_momentum": centred(key_of[6], (N_TP, ROWS, KVW), 0.1, 1.5, ((0, 16), (1, 16)), jnp.float32),
    }


beta_one = 0.9
beta_two = 0.999
inner_rate = 0.2
decay_rate = 0.1
outer_rate = 0.7
outer_mu = 0.9
adam_eps = 1e-08

def replica_step(total, inputs):
    rows, goal, weight, moment_a, moment_b = inputs
    shards_h = jnp.transpose(rows.reshape(TOK, N_TP, ROWS), (1, 0, 2))
    shards_w = weight.reshape(N_TP, ROWS, KVW)

    def add_group(acc, pair):
        piece_h, piece_w = pair
        part = jnp.dot(piece_h, piece_w, preferred_element_type=jnp.float32).astype(jnp.bfloat16)
        part = lax.optimization_barrier(part)
        return (acc + part.astype(jnp.float32), None)
    output, unused = lax.scan(add_group, jnp.zeros((TOK, KVW), jnp.float32), (shards_h, shards_w))
    residual = (output - goal.astype(jnp.float32)).astype(jnp.bfloat16)
    grad = lax.dot_general(rows, residual, (((0,), (0,)), ((), ())), preferred_element_type=jnp.float32)
    moment_one = beta_one * moment_a + (1.0 - beta_one) * grad
    moment_two = beta_two * moment_b + (1.0 - beta_two) * grad * grad
    corr_one = 1.0 - beta_one ** 3
    corr_two = 1.0 - beta_two ** 3
    weight_f = weight.astype(jnp.float32)
    step_dir = moment_one / corr_one / (jnp.sqrt(moment_two / corr_two) + adam_eps)
    updated = weight_f - inner_rate * (step_dir + decay_rate * weight_f)
    return (total + updated, None)

def reference(hidden, target, inner_weight, first_moment, second_moment, anchor, outer_momentum):
    rows = hidden.reshape(REPS, TOK, D)
    goals = target.reshape(REPS, TOK, KVW)
    total, unused = lax.scan(replica_step, jnp.zeros((D, KVW), jnp.float32), (rows, goals, inner_weight, first_moment, second_moment))
    replica_mean = total / REPS
    anchor_flat = anchor.reshape(D, KVW)
    momentum_flat = outer_momentum.reshape(D, KVW)
    delta = anchor_flat - replica_mean
    momentum_new = outer_mu * momentum_flat + delta
    fragment = (anchor_flat - outer_rate * (delta + outer_mu * momentum_new)).astype(jnp.bfloat16)
    return (fragment, momentum_new.reshape(N_TP, ROWS, KVW))
```

```python
import jax
import jax.numpy as jnp
from jax import lax
from jax.experimental import pallas as pl
from jax.experimental.pallas import tpu as pltpu
from jax.sharding import PartitionSpec as P

beta_one = 0.9
beta_two = 0.999
inner_rate = 0.2
decay_rate = 0.1
outer_rate = 0.7
outer_mu = 0.9
adam_eps = 1e-08

f32 = jnp.float32
bf16 = jnp.bfloat16


CHIPS = [[chip * 2 + core for chip in range(8)] for core in range(2)]


def spread(x, axis, groups=None):
    return lax.all_to_all(x, axis, 0, 0, axis_index_groups=groups)


def swap(x, axis, mask):
    return lax.ppermute(x, axis, [(i, i ^ mask) for i in range(16)])


def turn(x, by):
    return lax.ppermute(x, "rep", [(i, i // 4 * 4 + (i + by) % 4) for i in range(16)])


def part(x, at, parts):
    size = x.shape[0] // parts
    return lax.dynamic_slice_in_dim(x, at * size, size, 0)


def residual_kernel(at_ref, parts_ref, goal_ref, wide_ref):
    total = parts_ref[0].astype(f32)
    for i in range(1, parts_ref.shape[0]):
        total = total + parts_ref[i].astype(f32)
    residual = (total - goal_ref[...].astype(f32)).astype(bf16)
    for i in range(wide_ref.shape[0]):
        wide_ref[i] = residual


def residual_copies(parts, target, at, steps=4):
    copies, rows, cols = parts.shape
    size = rows // steps
    return pl.pallas_call(
        residual_kernel,
        out_shape=jax.ShapeDtypeStruct(parts.shape, bf16),
        grid_spec=pltpu.PrefetchScalarGridSpec(
            num_scalar_prefetch=1,
            grid=(steps,),
            in_specs=[
                pl.BlockSpec((copies, size, cols), lambda i, at: (0, i, 0)),
                pl.BlockSpec((size, cols), lambda i, at: (at[0] * steps + i, 0)),
            ],
            out_specs=pl.BlockSpec((copies, size, cols), lambda i, at: (0, i, 0)),
        ),
        cost_estimate=pl.CostEstimate(flops=copies * rows * cols, bytes_accessed=4 * copies * rows * cols, transcendentals=0),
        name="residual",
    )(at.reshape(1).astype(jnp.int32), parts, target)


def scaled_part(x, at, parts, by):
    rows, cols = x.shape[0] // parts, x.shape[1]

    def kernel(at_ref, x_ref, out_ref):
        out_ref[...] = x_ref[...] * by

    return pl.pallas_call(
        kernel,
        out_shape=jax.ShapeDtypeStruct((rows, cols), x.dtype),
        grid_spec=pltpu.PrefetchScalarGridSpec(
            num_scalar_prefetch=1,
            grid=(1,),
            in_specs=[pl.BlockSpec((rows, cols), lambda i, at: (at[0], 0))],
            out_specs=pl.BlockSpec((rows, cols), lambda i, at: (0, 0)),
        ),
        cost_estimate=pl.CostEstimate(flops=rows * cols, bytes_accessed=8 * rows * cols, transcendentals=0),
        name="scaled_part",
    )(at.reshape(1).astype(jnp.int32), x)


def local(hidden, target, inner_weight, first_moment, second_moment, anchor, outer_momentum):
    weight = inner_weight[0]
    cols = weight.shape[1]
    tp, rep = lax.axis_index("tp"), lax.axis_index("rep")
    core, chip = tp % 2, tp // 2
    half = hidden.shape[0] // 2
    mine, other = part(hidden, core, 2), part(hidden, 1 - core, 2)

    give = part(weight, 1 - rep // 8, 2)
    got = swap(give, "rep", 12)
    w_x = part(weight, rep // 8, 2).astype(f32) + got.astype(f32)
    give = part(w_x, 1 - rep // 4 % 2, 2)
    got = swap(give, "rep", 4)
    w_x = part(w_x, rep // 4 % 2, 2) + got
    w_sum = scaled_part(w_x, rep % 4, 4, 1.0 - inner_rate * decay_rate)
    for by in (2, 1, 3):
        give = part(w_x, (rep + by) % 4, 4)
        got = turn(give, by)
        w_sum = w_sum + got * (1.0 - inner_rate * decay_rate)

    w_other = swap(weight, "tp", 1)
    h_other = swap(other, "tp", 1)
    own = jnp.dot(mine, weight, preferred_element_type=f32)
    pair_sum = (own + jnp.dot(h_other, w_other, preferred_element_type=f32)).astype(bf16)
    parts = spread(pair_sum.reshape(8, half // 8, cols), "tp", CHIPS)
    wide = residual_copies(parts, target, core * 8 + chip)
    res = spread(wide, "tp", CHIPS).reshape(half, cols)
    dims = (((0,), (0,)), ((), ()))
    corr_one = 1.0 - beta_one**3
    corr_two = 1.0 - beta_two**3
    res_other = swap(res, "tp", 1)
    grad = lax.dot_general(mine, res, dims, preferred_element_type=f32)
    grad = grad + lax.dot_general(other, res_other, dims, preferred_element_type=f32)
    moment_one = beta_one * first_moment[0] + (1.0 - beta_one) * grad
    moment_two = beta_two * second_moment[0] + (1.0 - beta_two) * grad * grad
    step_dir = (moment_one / corr_one / (jnp.sqrt(moment_two / corr_two) + adam_eps)).astype(bf16)
    steps = spread(step_dir.reshape(16, 32, cols), "rep")
    updated = w_sum - inner_rate * jnp.sum(steps.astype(f32), axis=0)
    anchor_rows = anchor[0]
    delta = anchor_rows - updated / 16.0
    momentum_new = outer_mu * outer_momentum[0] + delta
    piece = (anchor_rows - outer_rate * (delta + outer_mu * momentum_new)).astype(bf16)
    wide = jnp.broadcast_to(piece[None], (16,) + piece.shape)
    fragment = spread(wide, "rep").reshape(512, cols)
    return (fragment, momentum_new[None])


def solution(mesh):
    placed = (
        P("rep", "tp"),
        P("rep", None),
        P("rep", "tp", None),
        P("rep", "tp", None),
        P("rep", "tp", None),
        P("tp", "rep", None),
        P("tp", "rep", None),
    )

    return jax.shard_map(
        local,
        mesh=mesh,
        in_specs=placed,
        out_specs=(P("tp", None), P("tp", "rep", None)),
        check_vma=False,
    )
```

```python
import jax
import jax.numpy as jnp
from jax import lax
from jax.experimental import pallas as pl
from jax.experimental.pallas import tpu as pltpu
from jax.sharding import PartitionSpec as P

beta_one = 0.9
beta_two = 0.999
inner_rate = 0.2
decay_rate = 0.1
outer_rate = 0.7
outer_mu = 0.9
adam_eps = 1e-08

f32 = jnp.float32
bf16 = jnp.bfloat16


ROWS = [[x * 4 + z for x in range(4)] for z in range(4)]
COLUMNS = [[x * 4 + z for z in range(4)] for x in range(4)]
CHIPS = [[chip * 2 + core for chip in range(8)] for core in range(2)]


def spread(x, axis, groups=None):
    return lax.all_to_all(x, axis, 0, 0, axis_index_groups=groups)


def swap(x, axis, mask):
    return lax.ppermute(x, axis, [(i, i ^ mask) for i in range(16)])


def turn(x, by):
    return lax.ppermute(x, "rep", [(i, i // 4 * 4 + (i + by) % 4) for i in range(16)])


def part(x, at, parts):
    size = x.shape[0] // parts
    return lax.dynamic_slice_in_dim(x, at * size, size, 0)


def residual_kernel(at_ref, parts_ref, goal_ref, wide_ref):
    total = parts_ref[0].astype(f32)
    for i in range(1, parts_ref.shape[0]):
        total = total + parts_ref[i].astype(f32)
    residual = (total - goal_ref[...].astype(f32)).astype(bf16)
    for i in range(wide_ref.shape[0]):
        wide_ref[i] = residual


def residual_copies(parts, target, at, steps=2):
    copies, rows, cols = parts.shape
    size = rows // steps
    return pl.pallas_call(
        residual_kernel,
        out_shape=jax.ShapeDtypeStruct(parts.shape, bf16),
        grid_spec=pltpu.PrefetchScalarGridSpec(
            num_scalar_prefetch=1,
            grid=(steps,),
            in_specs=[
                pl.BlockSpec((copies, size, cols), lambda i, at: (0, i, 0)),
                pl.BlockSpec((size, cols), lambda i, at: (at[0] * steps + i, 0)),
            ],
            out_specs=pl.BlockSpec((copies, size, cols), lambda i, at: (0, i, 0)),
        ),
        cost_estimate=pl.CostEstimate(flops=copies * rows * cols, bytes_accessed=4 * copies * rows * cols, transcendentals=0),
        name="residual",
    )(at.reshape(1).astype(jnp.int32), parts, target)


def summed_parts(x, got, side, at, by):
    rows, cols = got.shape
    size = rows // 4

    def kernel(at_ref, x_ref, got_ref, own_ref, *part_refs):
        def total(turned):
            start = pl.multiple_of((at_ref[1] + turned) % 4 * size, size)
            return x_ref[pl.ds(start, size), :] + got_ref[pl.ds(start, size), :]

        own_ref[...] = total(0) * by
        for turned, part_ref in enumerate(part_refs):
            part_ref[...] = total(turned + 1)

    piece = jax.ShapeDtypeStruct((size, cols), f32)
    return pl.pallas_call(
        kernel,
        out_shape=(piece,) * 4,
        grid_spec=pltpu.PrefetchScalarGridSpec(
            num_scalar_prefetch=1,
            grid=(1,),
            in_specs=[
                pl.BlockSpec((rows, cols), lambda i, at: (at[0], 0)),
                pl.BlockSpec((rows, cols), lambda i, at: (0, 0)),
            ],
            out_specs=(pl.BlockSpec((size, cols), lambda i, at: (0, 0)),) * 4,
        ),
        cost_estimate=pl.CostEstimate(flops=rows * cols, bytes_accessed=12 * rows * cols, transcendentals=0),
        name="summed_parts",
    )(jnp.stack([side, at]).astype(jnp.int32), x, got)


def local(hidden, target, inner_weight, first_moment, second_moment, anchor, outer_momentum):
    weight = inner_weight[0]
    cols = weight.shape[1]
    tp, rep = lax.axis_index("tp"), lax.axis_index("rep")
    core, chip = tp % 2, tp // 2
    half = hidden.shape[0] // 2
    mine, other = part(hidden, core, 2), part(hidden, 1 - core, 2)

    give = part(weight, 1 - rep // 8, 2)
    got = swap(give, "rep", 12)
    w_x = part(weight, rep // 8, 2).astype(f32) + got.astype(f32)
    give = part(w_x, 1 - rep // 4 % 2, 2)
    got = swap(give, "rep", 4)
    w_sum, *gives = summed_parts(w_x, got, rep // 4 % 2, rep % 4, 1.0 - inner_rate * decay_rate)
    for by in (2, 1, 3):
        got = turn(gives[by - 1], by)
        w_sum = w_sum + got * (1.0 - inner_rate * decay_rate)
    w_other = swap(weight, "tp", 1)
    h_other = swap(other, "tp", 1)
    own = jnp.dot(mine, weight, preferred_element_type=f32).astype(bf16)
    pair_sum = (own.astype(f32) + jnp.dot(h_other, w_other, preferred_element_type=f32)).astype(bf16)
    parts = spread(pair_sum.reshape(8, half // 8, cols), "tp", CHIPS)
    wide = residual_copies(parts, target, core * 8 + chip)
    res = spread(wide, "tp", CHIPS).reshape(half, cols)
    dims = (((0,), (0,)), ((), ()))
    corr_one = 1.0 - beta_one**3
    corr_two = 1.0 - beta_two**3
    res_other = swap(res, "tp", 1)
    grad = lax.dot_general(mine, res, dims, preferred_element_type=f32)
    grad = grad + lax.dot_general(other, res_other, dims, preferred_element_type=f32)
    moment_one = beta_one * first_moment[0] + (1.0 - beta_one) * grad
    moment_two = beta_two * second_moment[0] + (1.0 - beta_two) * grad * grad
    step_dir = (moment_one / corr_one / (jnp.sqrt(moment_two / corr_two) + adam_eps)).astype(bf16)
    steps = spread(step_dir.reshape(4, 128, cols), "rep", ROWS)
    step_sum = jnp.sum(steps.astype(f32), axis=0)
    steps = spread(step_sum.astype(bf16).reshape(4, 32, cols), "rep", COLUMNS)
    step_sum = jnp.sum(steps.astype(f32), axis=0)
    updated = w_sum - inner_rate * step_sum
    anchor_rows = anchor[0]
    delta = anchor_rows - updated / 16.0
    momentum_new = outer_mu * outer_momentum[0] + delta
    piece = (anchor_rows - outer_rate * (delta + outer_mu * momentum_new)).astype(bf16)
    wide = jnp.broadcast_to(piece[None], (4,) + piece.shape)
    piece = spread(wide, "rep", COLUMNS).reshape(128, cols)
    wide = jnp.broadcast_to(piece[None], (4,) + piece.shape)
    fragment = spread(wide, "rep", ROWS).reshape(512, cols)
    return (fragment, momentum_new[None])


def solution(mesh):
    placed = (
        P("rep", "tp"),
        P("rep", None),
        P("rep", "tp", None),
        P("rep", "tp", None),
        P("rep", "tp", None),
        P("tp", "rep", None),
        P("tp", "rep", None),
    )

    return jax.shard_map(
        local,
        mesh=mesh,
        in_specs=placed,
        out_specs=(P("tp", None), P("tp", "rep", None)),
        check_vma=False,
    )
```

```python
import jax
import jax.numpy as jnp
from jax import lax
from jax.experimental import pallas as pl
from jax.experimental.pallas import tpu as pltpu
from jax.sharding import PartitionSpec as P

beta_one = 0.9
beta_two = 0.999
inner_rate = 0.2
decay_rate = 0.1
outer_rate = 0.7
outer_mu = 0.9
adam_eps = 1e-08

f32 = jnp.float32
bf16 = jnp.bfloat16


ROWS = [[x * 4 + z for x in range(4)] for z in range(4)]
COLUMNS = [[x * 4 + z for z in range(4)] for x in range(4)]
CHIPS = [[chip * 2 + core for chip in range(8)] for core in range(2)]


def spread(x, axis, groups=None):
    return lax.all_to_all(x, axis, 0, 0, axis_index_groups=groups)


def swap(x, axis, mask):
    return lax.ppermute(x, axis, [(i, i ^ mask) for i in range(16)])


def turn(x, by):
    return lax.ppermute(x, "rep", [(i, i // 4 * 4 + (i + by) % 4) for i in range(16)])


def part(x, at, parts):
    size = x.shape[0] // parts
    return lax.dynamic_slice_in_dim(x, at * size, size, 0)


def residual_kernel(at_ref, parts_ref, goal_ref, wide_ref):
    total = parts_ref[0].astype(f32)
    for i in range(1, parts_ref.shape[0]):
        total = total + parts_ref[i].astype(f32)
    residual = (total - goal_ref[...].astype(f32)).astype(bf16)
    for i in range(wide_ref.shape[0]):
        wide_ref[i] = residual


def residual_copies(parts, target, at, steps=2):
    copies, rows, cols = parts.shape
    size = rows // steps
    return pl.pallas_call(
        residual_kernel,
        out_shape=jax.ShapeDtypeStruct(parts.shape, bf16),
        grid_spec=pltpu.PrefetchScalarGridSpec(
            num_scalar_prefetch=1,
            grid=(steps,),
            in_specs=[
                pl.BlockSpec((copies, size, cols), lambda i, at: (0, i, 0)),
                pl.BlockSpec((size, cols), lambda i, at: (at[0] * steps + i, 0)),
            ],
            out_specs=pl.BlockSpec((copies, size, cols), lambda i, at: (0, i, 0)),
        ),
        cost_estimate=pl.CostEstimate(flops=copies * rows * cols, bytes_accessed=4 * copies * rows * cols, transcendentals=0),
        name="residual",
    )(at.reshape(1).astype(jnp.int32), parts, target)


def summed_parts(x, got, side, at, by):
    rows, cols = got.shape
    size = rows // 4

    def kernel(at_ref, x_ref, got_ref, own_ref, *part_refs):
        def total(turned):
            start = pl.multiple_of((at_ref[1] + turned) % 4 * size, size)
            return x_ref[pl.ds(start, size), :] + got_ref[pl.ds(start, size), :]

        own_ref[...] = total(0) * by
        for turned, part_ref in enumerate(part_refs):
            part_ref[...] = total(turned + 1)

    piece = jax.ShapeDtypeStruct((size, cols), f32)
    return pl.pallas_call(
        kernel,
        out_shape=(piece,) * 4,
        grid_spec=pltpu.PrefetchScalarGridSpec(
            num_scalar_prefetch=1,
            grid=(1,),
            in_specs=[
                pl.BlockSpec((rows, cols), lambda i, at: (at[0], 0)),
                pl.BlockSpec((rows, cols), lambda i, at: (0, 0)),
            ],
            out_specs=(pl.BlockSpec((size, cols), lambda i, at: (0, 0)),) * 4,
        ),
        cost_estimate=pl.CostEstimate(flops=rows * cols, bytes_accessed=12 * rows * cols, transcendentals=0),
        name="summed_parts",
    )(jnp.stack([side, at]).astype(jnp.int32), x, got)


def local(hidden, target, inner_weight, first_moment, second_moment, anchor, outer_momentum):
    weight = inner_weight[0]
    cols = weight.shape[1]
    tp, rep = lax.axis_index("tp"), lax.axis_index("rep")
    core, chip = tp % 2, tp // 2
    half = hidden.shape[0] // 2
    mine, other = part(hidden, core, 2), part(hidden, 1 - core, 2)

    give = part(weight, 1 - rep // 8, 2)
    got = swap(give, "rep", 12)
    w_x = part(weight, rep // 8, 2).astype(f32) + got.astype(f32)
    give = part(w_x, 1 - rep // 4 % 2, 2)
    got = swap(give, "rep", 4)
    w_sum, *gives = summed_parts(w_x, got, rep // 4 % 2, rep % 4, 1.0 - inner_rate * decay_rate)
    turned = []
    for by in (2, 1, 3):
        turned.append(turn(gives[by - 1], by))
    w_sum = lax.optimization_barrier(w_sum + (turned[0] + turned[1] + turned[2]) * (1.0 - inner_rate * decay_rate))
    w_other = swap(weight, "tp", 1)
    h_other = swap(other, "tp", 1)
    own = jnp.dot(mine, weight, preferred_element_type=f32).astype(bf16)
    pair_sum = (own.astype(f32) + jnp.dot(h_other, w_other, preferred_element_type=f32)).astype(bf16)
    parts = spread(pair_sum.reshape(8, half // 8, cols), "tp", CHIPS)
    wide = residual_copies(parts, target, core * 8 + chip)
    res = spread(wide, "tp", CHIPS).reshape(half, cols)
    dims = (((0,), (0,)), ((), ()))
    corr_one = 1.0 - beta_one**3
    corr_two = 1.0 - beta_two**3
    res_other = swap(res, "tp", 1)
    grad = lax.dot_general(mine, res, dims, preferred_element_type=f32)
    grad = grad + lax.dot_general(other, res_other, dims, preferred_element_type=f32)
    moment_one = beta_one * first_moment[0] + (1.0 - beta_one) * grad
    moment_two = beta_two * second_moment[0] + (1.0 - beta_two) * grad * grad
    step_dir = (moment_one / corr_one / (jnp.sqrt(moment_two / corr_two) + adam_eps)).astype(bf16)
    steps = spread(step_dir.reshape(4, 128, cols), "rep", ROWS)
    step_sum = jnp.sum(steps.astype(f32), axis=0)
    steps = spread(step_sum.astype(bf16).reshape(4, 32, cols), "rep", COLUMNS)
    step_sum = jnp.sum(steps.astype(f32), axis=0)
    updated = w_sum - inner_rate * step_sum
    anchor_rows = anchor[0]
    delta = anchor_rows - updated / 16.0
    momentum_new = outer_mu * outer_momentum[0] + delta
    piece = (anchor_rows - outer_rate * (delta + outer_mu * momentum_new)).astype(bf16)
    wide = jnp.broadcast_to(piece[None], (4,) + piece.shape)
    piece = spread(wide, "rep", COLUMNS).reshape(128, cols)
    wide = jnp.broadcast_to(piece[None], (4,) + piece.shape)
    fragment = spread(wide, "rep", ROWS).reshape(512, cols)
    return (fragment, momentum_new[None])


def solution(mesh):
    placed = (
        P("rep", "tp"),
        P("rep", None),
        P("rep", "tp", None),
        P("rep", "tp", None),
        P("rep", "tp", None),
        P("tp", "rep", None),
        P("tp", "rep", None),
    )

    return jax.shard_map(
        local,
        mesh=mesh,
        in_specs=placed,
        out_specs=(P("tp", None), P("tp", "rep", None)),
        check_vma=False,
    )
```

```python
import jax
import jax.numpy as jnp
from jax import lax
from jax.experimental import pallas as pl
from jax.experimental.pallas import tpu as pltpu
from jax.sharding import PartitionSpec as P

beta_one = 0.9
beta_two = 0.999
inner_rate = 0.2
decay_rate = 0.1
outer_rate = 0.7
outer_mu = 0.9
adam_eps = 1e-08

f32 = jnp.float32
bf16 = jnp.bfloat16


ROWS = [[x * 4 + z for x in range(4)] for z in range(4)]
COLUMNS = [[x * 4 + z for z in range(4)] for x in range(4)]
CHIPS = [[chip * 2 + core for chip in range(8)] for core in range(2)]


def spread(x, axis, groups=None):
    return lax.all_to_all(x, axis, 0, 0, axis_index_groups=groups)


def swap(x, axis, mask):
    return lax.ppermute(x, axis, [(i, i ^ mask) for i in range(16)])


def turn(x, by):
    return lax.ppermute(x, "rep", [(i, i // 4 * 4 + (i + by) % 4) for i in range(16)])


def shift(x, by):
    return lax.ppermute(x, "rep", [(i, (i + 4 * by) % 16) for i in range(16)])


def part(x, at, parts):
    size = x.shape[0] // parts
    return lax.dynamic_slice_in_dim(x, at * size, size, 0)


def residual_kernel(at_ref, parts_ref, goal_ref, wide_ref):
    total = parts_ref[0].astype(f32)
    for i in range(1, parts_ref.shape[0]):
        total = total + parts_ref[i].astype(f32)
    residual = (total - goal_ref[...].astype(f32)).astype(bf16)
    for i in range(wide_ref.shape[0]):
        wide_ref[i] = residual


def residual_copies(parts, target, at, steps=2):
    copies, rows, cols = parts.shape
    size = rows // steps
    return pl.pallas_call(
        residual_kernel,
        out_shape=jax.ShapeDtypeStruct(parts.shape, bf16),
        grid_spec=pltpu.PrefetchScalarGridSpec(
            num_scalar_prefetch=1,
            grid=(steps,),
            in_specs=[
                pl.BlockSpec((copies, size, cols), lambda i, at: (0, i, 0)),
                pl.BlockSpec((size, cols), lambda i, at: (at[0] * steps + i, 0)),
            ],
            out_specs=pl.BlockSpec((copies, size, cols), lambda i, at: (0, i, 0)),
        ),
        cost_estimate=pl.CostEstimate(flops=copies * rows * cols, bytes_accessed=4 * copies * rows * cols, transcendentals=0),
        name="residual",
    )(at.reshape(1).astype(jnp.int32), parts, target)


def summed_parts(x, gots, block, at, by):
    rows, cols = gots[0].shape
    size = rows // 4

    def kernel(at_ref, *refs):
        ins, own_ref, part_refs = refs[:4], refs[4], refs[5:]

        def total(turned):
            start = pl.multiple_of((at_ref[1] + turned) % 4 * size, size)
            values = [ref[pl.ds(start, size), :].astype(f32) for ref in ins]
            return (values[0] + values[1]) + (values[2] + values[3])

        own_ref[...] = total(0) * by
        for turned, part_ref in enumerate(part_refs):
            part_ref[...] = total(turned + 1)

    piece = jax.ShapeDtypeStruct((size, cols), f32)
    whole = pl.BlockSpec((rows, cols), lambda i, at: (0, 0))
    return pl.pallas_call(
        kernel,
        out_shape=(piece,) * 4,
        grid_spec=pltpu.PrefetchScalarGridSpec(
            num_scalar_prefetch=1,
            grid=(1,),
            in_specs=[pl.BlockSpec((rows, cols), lambda i, at: (at[0], 0)), whole, whole, whole],
            out_specs=(pl.BlockSpec((size, cols), lambda i, at: (0, 0)),) * 4,
        ),
        cost_estimate=pl.CostEstimate(flops=4 * rows * cols, bytes_accessed=12 * rows * cols, transcendentals=0),
        name="summed_parts",
    )(jnp.stack([block, at]).astype(jnp.int32), x, *gots)


def local(hidden, target, inner_weight, first_moment, second_moment, anchor, outer_momentum):
    weight = inner_weight[0]
    cols = weight.shape[1]
    tp, rep = lax.axis_index("tp"), lax.axis_index("rep")
    core, chip = tp % 2, tp // 2
    half = hidden.shape[0] // 2
    mine, other = part(hidden, core, 2), part(hidden, 1 - core, 2)

    gots = []
    for by in (2, 1, 3):
        give = part(weight, (rep // 4 + by) % 4, 4)
        gots.append(shift(give, by))
    w_sum, *gives = summed_parts(weight, gots, rep // 4, rep % 4, 1.0 - inner_rate * decay_rate)
    turned = []
    for by in (2, 1, 3):
        turned.append(turn(gives[by - 1], by))
    w_sum = lax.optimization_barrier(w_sum + (turned[0] + turned[1] + turned[2]) * (1.0 - inner_rate * decay_rate))
    w_other = swap(weight, "tp", 1)
    h_other = swap(other, "tp", 1)
    own = jnp.dot(mine, weight, preferred_element_type=f32).astype(bf16)
    pair_sum = (own.astype(f32) + jnp.dot(h_other, w_other, preferred_element_type=f32)).astype(bf16)
    parts = spread(pair_sum.reshape(8, half // 8, cols), "tp", CHIPS)
    wide = residual_copies(parts, target, core * 8 + chip)
    res = spread(wide, "tp", CHIPS).reshape(half, cols)
    dims = (((0,), (0,)), ((), ()))
    corr_one = 1.0 - beta_one**3
    corr_two = 1.0 - beta_two**3
    res_other = swap(res, "tp", 1)
    grad = lax.dot_general(mine, res, dims, preferred_element_type=f32)
    grad = grad + lax.dot_general(other, res_other, dims, preferred_element_type=f32)
    moment_one = beta_one * first_moment[0] + (1.0 - beta_one) * grad
    moment_two = beta_two * second_moment[0] + (1.0 - beta_two) * grad * grad
    step_dir = (moment_one / corr_one / (jnp.sqrt(moment_two / corr_two) + adam_eps)).astype(bf16)
    steps = spread(step_dir.reshape(4, 128, cols), "rep", ROWS)
    step_sum = jnp.sum(steps.astype(f32), axis=0)
    steps = spread(step_sum.astype(bf16).reshape(4, 32, cols), "rep", COLUMNS)
    step_sum = jnp.sum(steps.astype(f32), axis=0)
    updated = w_sum - inner_rate * step_sum
    anchor_rows = anchor[0]
    delta = anchor_rows - updated / 16.0
    momentum_new = outer_mu * outer_momentum[0] + delta
    piece = (anchor_rows - outer_rate * (delta + outer_mu * momentum_new)).astype(bf16)
    wide = jnp.broadcast_to(piece[None], (4,) + piece.shape)
    piece = spread(wide, "rep", COLUMNS).reshape(128, cols)
    wide = jnp.broadcast_to(piece[None], (4,) + piece.shape)
    fragment = spread(wide, "rep", ROWS).reshape(512, cols)
    return (fragment, momentum_new[None])


def solution(mesh):
    placed = (
        P("rep", "tp"),
        P("rep", None),
        P("rep", "tp", None),
        P("rep", "tp", None),
        P("rep", "tp", None),
        P("tp", "rep", None),
        P("tp", "rep", None),
    )

    return jax.shard_map(
        local,
        mesh=mesh,
        in_specs=placed,
        out_specs=(P("tp", None), P("tp", "rep", None)),
        check_vma=False,
    )
```
